32 devices in a mesh: elem: 8 (over z, y), dir: 4 (over x, core).
Axes of the slice: x: 2, y: 2, z: 4, core: 2. Of those that a mesh axis runs over, the one named last changes fastest.
Arguments:
- history: bfloat16 [8, 32, 3072], P(None, 'dir', 'elem'), may hold values from -6 to 6
- incident: bfloat16 [2, 32, 3072], P(None, 'dir', 'elem'), may hold values from -6 to 6
- ztiles: bfloat16 [24, 32, 128, 128], P('elem'), may hold values from -0.09375 to 0.09375
- zinv: bfloat16 [24, 128, 128], P('elem'), may hold values from -0.5 to 0.5
- columns: int32 [24, 32], P('elem'), may hold values from 0 to 23, as said below
- lags: int32 [24, 32], P('elem'), may hold values from 1 to 8
- counts: int32 [24], P('elem'), may hold values from 8 to 32
- basis: bfloat16 [3072, 256], P('elem'), may hold values from -0.15625 to 0.15625
Outputs:
- densities: bfloat16 [2, 32, 3072], P(None, 'dir', 'elem')
- far_field: float32 [2, 32, 256], P(None, 'dir', 'elem')
The draws below stay inside these ranges and needn't reach their ends.
Inputs may be any that keep to these rules, and one draw needn't show every extreme that they name: A block row's slots at or beyond counts are unused; a source block may repeat within a row. `columns`: all slots, used or not, of the block rows of one index of elem name blocks whose panels lie on any one index of elem at most 12 times, and exactly 12 times for some index.
All inputs are finite; a program needn't handle non-finite values.
Results may differ from the reference program's by a relative error of at most 0.005.
Values may be sent and summed in bfloat16 or wider, within the bound.
A program may use at most 64 MiB of HBM per device.

```python
import jax
import jax.numpy as jnp

PAN_DEV = 384
BLK = 128
K_MAX = 32
L = 8
DIRS = 32
SH = 256
STEPS = 2
PANELS = 3072
NBLK = 24
CAP = 12


def draw_columns(key, part):
    rows_dev = PAN_DEV // BLK
    devices_elem = NBLK // rows_dev
    slots_dev = rows_dev * K_MAX

    def one_device(dev_key):
        key_slots = jax.random.fold_in(dev_key, 11)
        key_owner = jax.random.fold_in(dev_key, 12)
        key_local = jax.random.fold_in(dev_key, 13)
        slot_order = jax.random.permutation(key_slots, slots_dev)
        owner_order = jax.random.permutation(key_owner, devices_elem)
        owner = owner_order[slot_order // CAP]
        local = jax.random.randint(key_local, (slots_dev,), 0, rows_dev)
        return (owner * rows_dev + local).astype(jnp.int32)
    dev_keys = jax.vmap(lambda index: jax.random.fold_in(key, index))(jnp.arange(devices_elem))
    blocks = jax.vmap(one_device)(dev_keys)
    return blocks.reshape(NBLK, K_MAX).astype(jnp.int32)


def set_ends(array, own_key, smallest, largest):
    spot = [jax.random.randint(jax.random.fold_in(own_key, axis), (), 0, length) for axis, length in enumerate(array.shape)]
    longest = array.shape.index(max(array.shape))
    beside = spot[:longest] + [(spot[longest] + 1) % array.shape[longest]] + spot[longest + 1:]
    return array.at[tuple(spot)].set(smallest).at[tuple(beside)].set(largest)


def strengthened(values, key, source, target, shards_of, factor):
    def block_of(axis_at):
        return (jnp.arange(values.shape[axis_at]) // (values.shape[axis_at] // shards_of)).reshape((-1,) + (1,) * (values.ndim - 1 - axis_at))

    first = jax.random.permutation(key, shards_of)[block_of(target)]
    second = (block_of(target) + shards_of // 2) % shards_of
    return jnp.where((block_of(source) == first) | (block_of(source) == second), factor * values, values)


def block_levels(own_key, shape, pieces, smallest, largest):
    def one(dim, parts):
        heights = jax.random.uniform(jax.random.fold_in(jax.random.fold_in(own_key, 6), dim), (parts,), jnp.float32, smallest / len(pieces), largest / len(pieces))
        return jnp.repeat(jnp.exp(heights), shape[dim] // parts).reshape((-1,) + (1,) * (len(shape) - dim - 1))

    loudness = one(*pieces[0])
    for cut in pieces[1:]:
        loudness = loudness * one(*cut)
    return loudness


def bell_draw(stream_key, shape, spread, most, pieces=(), held_as=jnp.bfloat16):
    drawn = jax.random.normal(stream_key, shape, jnp.float32) * spread
    if len(pieces) > 0:
        drawn = block_levels(stream_key, shape, pieces, -0.22, 0.18) * drawn
    return jnp.clip(drawn, min=-most, max=most).astype(held_as)


def bell_draw_with(rng, extent, scale, most, split, heavy, kind=jnp.bfloat16):
    result = scale * jax.random.normal(rng, extent, jnp.float32)
    if split:
        result = result * block_levels(rng, extent, split, -0.22, 0.18)
    return jnp.clip(strengthened(result, jax.random.fold_in(rng, 3), *heavy), -most, most).astype(kind)


def setup_inputs(seed: int = 0) -> dict:
    key_of = jax.random.split(jax.random.key(seed), 9)
    return {
        "history": bell_draw(key_of[0], (L, DIRS, PANELS), 1.0, 6.0, ((1, 4), (2, 8))),
        "incident": bell_draw(key_of[1], (STEPS, DIRS, PANELS), 1.0, 6.0, ((1, 4), (2, 8))),
        "ztiles": bell_draw(key_of[2], (NBLK, K_MAX, BLK, BLK), (BLK * K_MAX) ** -0.5, 0.09375, ((0, 8),)),
        "zinv": bell_draw(key_of[3], (NBLK, BLK, BLK), BLK ** -0.5, 0.5, ((0, 8),)),
        "columns": draw_columns(jax.random.fold_in(key_of[8], 71), 0),
        "lags": set_ends(jax.random.randint(key_of[5], (NBLK, K_MAX), 1, L + 1), jax.random.fold_in(key_of[5], 1), 1, L).astype(jnp.int32),
        "counts": set_ends(jax.random.randint(key_of[6], (NBLK,), max(1, K_MAX // 4), K_MAX + 1), jax.random.fold_in(key_of[6], 1), max(1, K_MAX // 4), K_MAX).astype(jnp.int32),
        "basis": bell_draw_with(key_of[7], (PANELS, SH), PANELS ** -0.5, 0.15625, ((0, 8),), (0, 1, 8, 2.0)),
    }


def reference(history, incident, ztiles, zinv, columns, lags, counts, basis):
    window = history
    slot_index = jnp.arange(K_MAX, dtype=jnp.int32)
    active = slot_index[None, :] < counts[:, None]
    dens_list = []
    far_list = []
    for step_index in range(STEPS):
        grid = window.reshape(L, DIRS, NBLK, BLK)
        picked = grid[lags - 1, :, columns, :]
        picked = jnp.where(active[:, :, None, None], picked, jnp.zeros((), picked.dtype))
        history_sum = jnp.einsum('rkdj,rkji->dri', picked.astype(jnp.float32), ztiles.astype(jnp.float32))
        own = incident[step_index].astype(jnp.float32).reshape(DIRS, NBLK, BLK)
        source = (own - history_sum).astype(jnp.bfloat16)
        density = jnp.einsum('drj,rji->dri', source.astype(jnp.float32), zinv.astype(jnp.float32))
        density = density.reshape(DIRS, PANELS).astype(jnp.bfloat16)
        far_part = jnp.dot(density, basis, preferred_element_type=jnp.float32)
        dens_list.append(density)
        far_list.append(far_part)
        window = jnp.concatenate([density[None], window[:-1]], axis=0)
    return jnp.stack(dens_list), jnp.stack(far_list)
```

```python
import functools

import jax
import jax.numpy as jnp
from jax import lax
from jax.experimental import pallas as pl
from jax.experimental.pallas import tpu as pltpu
from jax.sharding import PartitionSpec as P

MESH = pl.DeviceIdType.MESH
LANES = 128


def bit(value, place):
    return lax.rem(lax.div(value, 1 << place), 2)


def flip(value, mask):
    for place in range(mask.bit_length()):
        if mask >> place & 1:
            value = value + (1 << place) * (1 - 2 * bit(value, place))
    return value


def when(condition, body):
    if condition is True:
        body()
    elif condition is not False:
        pl.when(condition)(body)


def both(a, b):
    if a is False or b is False:
        return False
    if a is True:
        return b
    if b is True:
        return a
    return jnp.logical_and(a, b)


def march_kernel(n, hist_hbm, inc_hbm, z_hbm, zinv_hbm, basis_hbm, cols_hbm,
                 lags_hbm, counts_hbm,
                 dens_out, far_out,
                 ext, ztile, zinv, basis, inc, cols, lags, counts, picked, picked1, dens0, part, far_in,
                 load_sem, own_sem, ready, hist_send, hist_recv, relay_send, relay_recv,
                 cross_send, cross_recv, dens_send, dens_recv, far_send, far_recv):
    me = lax.axis_index("elem")
    rows, slots = cols.shape
    levels, dirs, width = hist_hbm.shape
    half = n // 2
    owned = far_out.shape[2]
    z, y = lax.div(me, 2), lax.rem(me, 2)
    partner = me + 1 - 2 * y
    barrier = pltpu.get_barrier_semaphore()
    tuned = half == 4
    top = half - 1
    crosses = both(tuned, both(z == half - 1, y == 1))
    crossed = both(tuned, both(z == 0, y == 0))
    opposite = flip(z, top) * 2 + 1 - y

    def line(k):
        return flip(z, k) * 2 + y

    def later(k):
        return bit(z, k.bit_length() - 1) == 0

    def signal(semaphore, target):
        pl.semaphore_signal(semaphore, inc=1, device_id={"elem": target}, device_id_type=MESH)

    earlier = y
    when(y == 0, lambda: signal(barrier, partner))
    for k in range(1, half):
        when(later(k), lambda: signal(barrier, line(k)))
        earlier = earlier + jnp.where(later(k), 0, 1)
    if tuned:
        when(crossed, lambda: signal(barrier, opposite))
        earlier = earlier + jnp.where(crosses, 1, 0)
    per = levels * rows
    own = [
        pltpu.make_async_copy(
            hist_hbm.at[:, :, pl.ds(row * LANES, LANES)],
            ext.at[pl.ds(me * per + row * levels, levels)], own_sem.at[row])
        for row in range(rows)]
    for copy in own:
        copy.start()
    when(me > 0, lambda: pl.semaphore_wait(barrier, earlier))
    when(y == 1, lambda: signal(ready.at[0], partner))
    for k in range(1, half):
        when(jnp.logical_not(later(k)), lambda: signal(ready.at[k], line(k)))

    def block_copy(block, target, send_sem, recv_sem):
        place = pl.ds(block * per, per)
        return pltpu.make_async_remote_copy(
            src_ref=ext.at[place], dst_ref=ext.at[place], send_sem=send_sem, recv_sem=recv_sem,
            device_id={"elem": target}, device_id_type=MESH)

    def along(k):
        target = partner if k == 0 else line(k)
        return block_copy(me, target, hist_send.at[k], hist_recv.at[k])

    def along_in(k):
        source = partner if k == 0 else line(k)
        return block_copy(source, partner, hist_send.at[k], hist_recv.at[k])

    def cross(block):
        return block_copy(block, opposite, cross_send, cross_recv)

    def relay(k):
        return block_copy(line(k), partner, relay_send.at[k], relay_recv.at[k])

    def relay_in(k):
        return block_copy(flip(z, k) * 2 + 1 - y, partner, relay_send.at[k], relay_recv.at[k])

    tables = [
        pltpu.make_async_copy(cols_hbm, cols, load_sem.at[0]),
        pltpu.make_async_copy(lags_hbm, lags, load_sem.at[5]),
        pltpu.make_async_copy(counts_hbm, counts, load_sem.at[6]),
    ]
    loads = [
        pltpu.make_async_copy(z_hbm, ztile, load_sem.at[1]),
        pltpu.make_async_copy(zinv_hbm, zinv, load_sem.at[2]),
        pltpu.make_async_copy(basis_hbm, basis, load_sem.at[3]),
        pltpu.make_async_copy(inc_hbm, inc, load_sem.at[4]),
    ]
    for copy in own:
        copy.wait()
    when(y == 1, lambda: along(0).start())
    for k in range(1, half):
        when(jnp.logical_not(later(k)), lambda: along(k).start())
    when(crosses, lambda: cross(me).start())
    for load in tables + loads:
        load.start()

    middle = lax.rem(bit(z, 0) + bit(z, 1), 2) == 1
    if tuned:
        outer = jnp.logical_not(middle)
        order = [(0, True), (1, True), (3, middle), (2, True), (3, outer)]
    else:
        order = [(k, True) for k in range(half)]
    for k, chosen in order:
        def answer():
            pl.semaphore_wait(ready.at[k], 1)
            along(k).start()
        when(both(chosen, y == 0 if k == 0 else later(k)), answer)

    ext[n * per] = jnp.zeros((dirs, LANES), ext.dtype)
    dens0[n * rows] = jnp.zeros((dirs, LANES), dens0.dtype)
    for load in tables:
        load.wait()
    place0, place1, from_dens = [], [], []
    for row in range(rows):
        live = counts[row]
        for slot in range(slots):
            column, lag = cols[row, slot], lags[row, slot]
            lag = jnp.where(slot < live, lag, 0)
            newest = column * levels + lag - 1
            place0.append(jnp.where(lag > 0, newest, n * per))
            place1.append(jnp.where(lag > 1, newest - 1, n * per))
            from_dens.append(jnp.where(lag == 1, column, n * rows))

    passes = {k: True for k in range(1, half)}
    if tuned:
        passes[top] = jnp.logical_not(both(z == 0, y == 1))
        first = z == 0
        order = [(1, True), (3, jnp.logical_not(first)), (2, True), (3, first)]
    else:
        order = [(k, True) for k in range(1, half)]
    for k, chosen in order:
        def pass_on():
            along_in(k).wait_recv()
            relay(k).start()
        when(both(chosen, passes[k]), pass_on)
    along_in(0).wait_recv()
    for k in range(1, half):
        if k == top and tuned:
            when(jnp.logical_not(passes[k]), lambda: along_in(k).wait_recv())
            when(crossed, lambda: cross(opposite).wait_recv())
            when(jnp.logical_not(crossed), lambda: relay_in(k).wait_recv())
        else:
            relay_in(k).wait_recv()
    for load in loads:
        load.wait()

    sums = []
    for row in range(rows):
        for slot in range(slots):
            at = row * slots + slot
            lanes = pl.ds(slot * LANES, LANES)
            picked[row, 0:dirs, lanes] = ext[place0[at]]
            picked[row, dirs:2 * dirs, lanes] = ext[place1[at]]
        sums.append(jnp.dot(picked[row], ztile[row], preferred_element_type=jnp.float32))

    def density_of(step, row, history_sum):
        own_field = inc[step, :, row * LANES:(row + 1) * LANES].astype(jnp.float32)
        source = (own_field - history_sum).astype(jnp.bfloat16)
        return jnp.dot(source, zinv[row], preferred_element_type=jnp.float32).astype(jnp.bfloat16)

    for row in range(rows):
        density = density_of(0, row, sums[row][0:dirs])
        dens0[me * rows + row] = density
        dens_out[0, :, row * LANES:(row + 1) * LANES] = density

    def send_density(mask):
        place = pl.ds(me * rows, rows)
        return pltpu.make_async_remote_copy(
            src_ref=dens0.at[place], dst_ref=dens0.at[place],
            send_sem=dens_send.at[mask], recv_sem=dens_recv.at[mask],
            device_id={"elem": flip(me, mask)}, device_id_type=MESH)

    masks = list(range(n - 1, 0, -1))
    dens_copies = [send_density(mask) for mask in masks]
    for copy in dens_copies:
        copy.start()

    def far_copies(step):
        copies = []
        for mask in masks:
            target = flip(me, mask)
            tile = target * owned // LANES
            copies.append(pltpu.make_async_remote_copy(
                src_ref=part.at[step, tile], dst_ref=far_in.at[step, mask],
                send_sem=far_send.at[step, mask], recv_sem=far_recv.at[step, mask],
                device_id={"elem": target}, device_id_type=MESH))
        return copies

    def far_parts(step, density):
        value = jnp.dot(density, basis[...], preferred_element_type=jnp.float32)
        for tile in range(part.shape[1]):
            part[step, tile] = value[:, tile * LANES:(tile + 1) * LANES]

    far_parts(0, dens_out[0])
    far0 = far_copies(0)
    for copy in far0:
        copy.start()

    for k in range(half):
        along(k).wait_send()
    for k in range(1, half):
        when(passes[k], lambda: relay(k).wait_send())
    when(crosses, lambda: cross(me).wait_send())

    for copy in dens_copies:
        copy.wait_recv()
    for row in range(rows):
        for slot in range(slots):
            picked1[row, :, pl.ds(slot * LANES, LANES)] = dens0[from_dens[row * slots + slot]]
        total = sums[row][dirs:2 * dirs] + jnp.dot(
            picked1[row], ztile[row], preferred_element_type=jnp.float32)
        dens_out[1, :, row * LANES:(row + 1) * LANES] = density_of(1, row, total)
    far_parts(1, dens_out[1])
    far1 = far_copies(1)
    for copy in far1:
        copy.start()
    for copy in dens_copies:
        copy.wait_send()
    shift = lax.rem(me * owned, LANES)
    for step, copies in ((0, far0), (1, far1)):
        for copy in copies:
            copy.wait_recv()
        total = part[step, me * owned // LANES]
        for mask in masks:
            total = total + far_in[step, mask]
        total = pltpu.roll(total, lax.rem(LANES - shift, LANES), 1)
        far_out[step] = total[:, 0:owned]
    for copy in far0 + far1:
        copy.wait_send()


def on_device(history, incident, ztiles, zinv, columns, lags, counts, basis, *, n):
    steps, dirs, width = incident.shape
    levels = history.shape[0]
    rows, slots, tile, _ = ztiles.shape
    coeffs = basis.shape[1]
    flat = ztiles.reshape(rows, slots * tile, tile)
    hbm = pl.BlockSpec(memory_space=pltpu.HBM)
    vmem = pl.BlockSpec(memory_space=pltpu.VMEM)
    bf16, f32 = jnp.bfloat16, jnp.float32
    dma = pltpu.SemaphoreType.DMA
    tiles = coeffs // LANES
    half = n // 2
    return pl.pallas_call(
        functools.partial(march_kernel, n),
        out_shape=(pltpu.VMEM((steps, dirs, width), bf16),
                   pltpu.VMEM((steps, dirs, coeffs // n), f32)),
        in_specs=[hbm] * 8,
        out_specs=(vmem, vmem),
        scratch_shapes=[
            pltpu.VMEM((n * levels * rows + 1, dirs, LANES), bf16),
            pltpu.VMEM(flat.shape, bf16),
            pltpu.VMEM(zinv.shape, bf16),
            pltpu.VMEM(basis.shape, bf16),
            pltpu.VMEM(incident.shape, bf16),
            pltpu.SMEM(columns.shape, jnp.int32),
            pltpu.SMEM(lags.shape, jnp.int32),
            pltpu.SMEM(counts.shape, jnp.int32),
            pltpu.VMEM((rows, 2 * dirs, slots * tile), bf16),
            pltpu.VMEM((rows, dirs, slots * tile), bf16),
            pltpu.VMEM((n * rows + 1, dirs, LANES), bf16),
            pltpu.VMEM((steps, tiles, dirs, LANES), f32),
            pltpu.VMEM((steps, n, dirs, LANES), f32),
            dma((7,)), dma((rows,)),
            pltpu.SemaphoreType.REGULAR((half,)),
            dma((half,)), dma((half,)), dma((half,)), dma((half,)),
            dma, dma,
            dma((n,)), dma((n,)),
            dma((steps, n)), dma((steps, n)),
        ],
        compiler_params=pltpu.CompilerParams(
            collective_id=0, has_side_effects=True, vmem_limit_bytes=32 * 1024 * 1024),
    )(*(pltpu.with_memory_space_constraint(x, pltpu.HBM)
        for x in (history, incident, flat, zinv, basis, columns, lags, counts)))


def solution(mesh):
    in_specs = (
        P(None, "dir", "elem"),
        P(None, "dir", "elem"),
        P("elem", None, None, None),
        P("elem", None, None),
        P("elem", None),
        P("elem", None),
        P("elem"),
        P("elem", None),
    )
    out_specs = (P(None, "dir", "elem"), P(None, "dir", "elem"))
    return jax.shard_map(
        functools.partial(on_device, n=mesh.shape["elem"]), mesh=mesh,
        in_specs=in_specs, out_specs=out_specs, check_vma=False)
```

```python
import functools

import jax
import jax.numpy as jnp
from jax import lax
from jax.experimental import pallas as pl
from jax.experimental.pallas import tpu as pltpu
from jax.sharding import PartitionSpec as P

MESH = pl.DeviceIdType.MESH
LANES = 128


def bit(value, place):
    return lax.rem(lax.div(value, 1 << place), 2)


def flip(value, mask):
    for place in range(mask.bit_length()):
        if mask >> place & 1:
            value = value + (1 << place) * (1 - 2 * bit(value, place))
    return value


def when(condition, body):
    if condition is True:
        body()
    elif condition is not False:
        pl.when(condition)(body)


def both(a, b):
    if a is False or b is False:
        return False
    if a is True:
        return b
    if b is True:
        return a
    return jnp.logical_and(a, b)


def march_kernel(n, hist_hbm, inc_hbm, z_hbm, zinv_hbm, basis_hbm, cols_hbm,
                 lags_hbm, counts_hbm,
                 dens_out, far_out,
                 ext, weights, basis, inc, slot_table, counts, picked, picked1, dens0, part, far_in,
                 own_sem, table_sem, load_sem, ready, line_recv, hist_recv, hist_send,
                 dens_recv, far_recv, late_send):
    me = lax.axis_index("elem")
    _, rows, slots = slot_table.shape
    levels, dirs, width = hist_hbm.shape
    half = n // 2
    owned = far_out.shape[2]
    z, y = lax.div(me, 2), lax.rem(me, 2)
    partner = me + 1 - 2 * y
    barrier = pltpu.get_barrier_semaphore()
    tuned = half == 4
    top = half - 1
    crosses = both(tuned, both(z == half - 1, y == 1))
    crossed = both(tuned, both(z == 0, y == 0))
    opposite = flip(z, top) * 2 + 1 - y

    def line(k):
        return flip(z, k) * 2 + y

    def later(k):
        return bit(z, k.bit_length() - 1) == 0

    def signal(semaphore, target):
        pl.semaphore_signal(semaphore, inc=1, device_id={"elem": target}, device_id_type=MESH)

    earlier = y
    when(y == 0, lambda: signal(barrier, partner))
    for k in range(1, half):
        when(later(k), lambda: signal(barrier, line(k)))
        earlier = earlier + jnp.where(later(k), 0, 1)
    if tuned:
        when(crossed, lambda: signal(barrier, opposite))
        earlier = earlier + jnp.where(crosses, 1, 0)
    per = levels * rows
    own = [
        pltpu.make_async_copy(
            hist_hbm.at[:, :, pl.ds(row * LANES, LANES)],
            ext.at[pl.ds(me * per + row * levels, levels)], own_sem)
        for row in range(rows)]
    for copy in own:
        copy.start()
    when(me > 0, lambda: pl.semaphore_wait(barrier, earlier))
    when(y == 1, lambda: signal(ready.at[0], partner))
    for k in range(1, half):
        when(jnp.logical_not(later(k)), lambda: signal(ready.at[k], line(k)))

    def block_copy(block, target, recv_sem, blocks=1):
        place = pl.ds(block * per, blocks * per)
        return pltpu.make_async_remote_copy(
            src_ref=ext.at[place], dst_ref=ext.at[place], send_sem=hist_send, recv_sem=recv_sem,
            device_id={"elem": target}, device_id_type=MESH)

    def along(k):
        return block_copy(me, line(k), line_recv.at[k - 1])

    def along_in(k):
        return block_copy(line(k), partner, line_recv.at[k - 1])

    to_partner = block_copy(me, partner, hist_recv)
    cross = block_copy(me, opposite, hist_recv)

    def relay(k):
        return block_copy(line(k), partner, hist_recv)

    def rest(blocks):
        return block_copy(0, partner, hist_recv, blocks)

    deep = z_hbm.shape[1]
    tables = [
        pltpu.make_async_copy(cols_hbm, slot_table.at[0], table_sem.at[0]),
        pltpu.make_async_copy(lags_hbm, slot_table.at[1], table_sem.at[0]),
        pltpu.make_async_copy(counts_hbm, counts, table_sem.at[1]),
    ]
    loads = [
        pltpu.make_async_copy(z_hbm, weights.at[:, pl.ds(0, deep)], load_sem.at[0]),
        pltpu.make_async_copy(zinv_hbm, weights.at[:, pl.ds(deep, LANES)], load_sem.at[0]),
        pltpu.make_async_copy(basis_hbm, basis, load_sem.at[1]),
        pltpu.make_async_copy(inc_hbm, inc, load_sem.at[2]),
    ]
    pltpu.make_async_copy(ext.at[pl.ds(0, per)], ext.at[pl.ds(0, per)], own_sem).wait()
    when(y == 1, lambda: to_partner.start())
    for k in range(1, half):
        when(jnp.logical_not(later(k)), lambda: along(k).start())
    when(crosses, lambda: cross.start())
    for load in tables + loads:
        load.start()

    middle = lax.rem(bit(z, 0) + bit(z, 1), 2) == 1
    if tuned:
        outer = jnp.logical_not(middle)
        order = [(0, True), (1, True), (3, middle), (2, True), (3, outer)]
    else:
        order = [(k, True) for k in range(half)]
    for k, chosen in order:
        def answer():
            pl.semaphore_wait(ready.at[k], 1)
            (to_partner if k == 0 else along(k)).start()
        when(both(chosen, y == 0 if k == 0 else later(k)), answer)

    ext[n * per] = jnp.zeros((dirs, LANES), ext.dtype)
    dens0[n * rows] = jnp.zeros((dirs, LANES), dens0.dtype)
    pltpu.make_async_copy(slot_table, slot_table, table_sem.at[0]).wait()
    tables[2].wait()
    place0, place1, from_dens = [], [], []
    for row in range(rows):
        live = counts[row]
        for slot in range(slots):
            column, lag = slot_table[0, row, slot], slot_table[1, row, slot]
            lag = jnp.where(slot < live, lag, 0)
            newest = column * levels + lag - 1
            place0.append(jnp.where(lag > 0, newest, n * per))
            place1.append(jnp.where(lag > 1, newest - 1, n * per))
            from_dens.append(jnp.where(lag == 1, column, n * rows))

    passes = {k: True for k in range(1, half)}
    if tuned:
        passes[top] = jnp.logical_not(both(z == 0, y == 1))
        first = z == 0
        order = [(1, True), (3, jnp.logical_not(first)), (2, True), (3, first)]
    else:
        order = [(k, True) for k in range(1, half)]
    for k, chosen in order:
        def pass_on():
            along_in(k).wait_recv()
            relay(k).start()
        when(both(chosen, passes[k]), pass_on)
    if tuned:
        when(jnp.logical_not(passes[top]), lambda: along_in(top).wait_recv())
    rest(half).wait_recv()
    pltpu.make_async_copy(weights, weights, load_sem.at[0]).wait()
    for load in loads[2:]:
        load.wait()

    sums = []
    for row in range(rows):
        for slot in range(slots):
            at = row * slots + slot
            lanes = pl.ds(slot * LANES, LANES)
            picked[row, 0:dirs, lanes] = ext[place0[at]]
            picked[row, dirs:2 * dirs, lanes] = ext[place1[at]]
        sums.append(jnp.dot(picked[row], weights[row, 0:deep], preferred_element_type=jnp.float32))

    def density_of(step, row, history_sum):
        own_field = inc[step, :, row * LANES:(row + 1) * LANES].astype(jnp.float32)
        source = (own_field - history_sum).astype(jnp.bfloat16)
        return jnp.dot(source, weights[row, deep:], preferred_element_type=jnp.float32).astype(jnp.bfloat16)

    for row in range(rows):
        density = density_of(0, row, sums[row][0:dirs])
        dens0[me * rows + row] = density
        dens_out[0, :, row * LANES:(row + 1) * LANES] = density

    def send_density(mask):
        place = pl.ds(me * rows, rows)
        return pltpu.make_async_remote_copy(
            src_ref=dens0.at[place], dst_ref=dens0.at[place], send_sem=late_send, recv_sem=dens_recv,
            device_id={"elem": flip(me, mask)}, device_id_type=MESH)

    masks = list(range(n - 1, 0, -1))
    for mask in masks:
        send_density(mask).start()

    def send_far(step):
        for mask in masks:
            target = flip(me, mask)
            pltpu.make_async_remote_copy(
                src_ref=part.at[step, target * owned // LANES], dst_ref=far_in.at[step * n + mask],
                send_sem=late_send, recv_sem=far_recv,
                device_id={"elem": target}, device_id_type=MESH).start()

    def arrived(buffer, count, semaphore):
        place = buffer.at[pl.ds(0, count)]
        pltpu.make_async_copy(place, place, semaphore).wait()

    def far_parts(step, density):
        value = jnp.dot(density, basis[...], preferred_element_type=jnp.float32)
        for tile in range(part.shape[1]):
            part[step, tile] = value[:, tile * LANES:(tile + 1) * LANES]

    far_parts(0, dens_out[0])
    send_far(0)
    arrived(dens0, (n - 1) * rows, dens_recv)
    for row in range(rows):
        for slot in range(slots):
            picked1[row, :, pl.ds(slot * LANES, LANES)] = dens0[from_dens[row * slots + slot]]
        total = sums[row][dirs:2 * dirs] + jnp.dot(
            picked1[row], weights[row, 0:deep], preferred_element_type=jnp.float32)
        dens_out[1, :, row * LANES:(row + 1) * LANES] = density_of(1, row, total)
    far_parts(1, dens_out[1])
    send_far(1)

    if tuned:
        fewer = jnp.logical_not(passes[top])
        when(crosses, lambda: rest(n).wait_send())
        when(fewer, lambda: rest(n - 2).wait_send())
        when(jnp.logical_not(jnp.logical_or(crosses, fewer)), lambda: rest(n - 1).wait_send())
    else:
        rest(n - 1).wait_send()

    shift = lax.rem(me * owned, LANES)
    steps = part.shape[0]
    arrived(far_in, steps * (n - 1), far_recv)
    for step in range(steps):
        total = part[step, me * owned // LANES]
        for mask in masks:
            total = total + far_in[step * n + mask]
        total = pltpu.roll(total, lax.rem(LANES - shift, LANES), 1)
        far_out[step] = total[:, 0:owned]
    arrived(ext, (n - 1) * (rows + 2 * steps), late_send)


def on_device(history, incident, ztiles, zinv, columns, lags, counts, basis, *, n):
    steps, dirs, width = incident.shape
    levels = history.shape[0]
    rows, slots, tile, _ = ztiles.shape
    coeffs = basis.shape[1]
    flat = ztiles.reshape(rows, slots * tile, tile)
    hbm = pl.BlockSpec(memory_space=pltpu.HBM)
    vmem = pl.BlockSpec(memory_space=pltpu.VMEM)
    bf16, f32 = jnp.bfloat16, jnp.float32
    dma = pltpu.SemaphoreType.DMA
    tiles = coeffs // LANES
    half = n // 2
    return pl.pallas_call(
        functools.partial(march_kernel, n),
        out_shape=(pltpu.VMEM((steps, dirs, width), bf16),
                   pltpu.VMEM((steps, dirs, coeffs // n), f32)),
        in_specs=[hbm] * 8,
        out_specs=(vmem, vmem),
        scratch_shapes=[
            pltpu.VMEM((n * levels * rows + 1, dirs, LANES), bf16),
            pltpu.VMEM((rows, (slots + 1) * tile, tile), bf16),
            pltpu.VMEM(basis.shape, bf16),
            pltpu.VMEM(incident.shape, bf16),
            pltpu.SMEM((2,) + columns.shape, jnp.int32),
            pltpu.SMEM(counts.shape, jnp.int32),
            pltpu.VMEM((rows, 2 * dirs, slots * tile), bf16),
            pltpu.VMEM((rows, dirs, slots * tile), bf16),
            pltpu.VMEM((n * rows + 1, dirs, LANES), bf16),
            pltpu.VMEM((steps, tiles, dirs, LANES), f32),
            pltpu.VMEM((steps * n, dirs, LANES), f32),
            dma, dma((2,)), dma((3,)),
            pltpu.SemaphoreType.REGULAR((half,)), dma((half - 1,)),
            dma, dma, dma, dma, dma,
        ],
        compiler_params=pltpu.CompilerParams(
            collective_id=0, has_side_effects=True, vmem_limit_bytes=32 * 1024 * 1024),
    )(*(pltpu.with_memory_space_constraint(x, pltpu.HBM)
        for x in (history, incident, flat, zinv, basis, columns, lags, counts)))


def solution(mesh):
    in_specs = (
        P(None, "dir", "elem"),
        P(None, "dir", "elem"),
        P("elem", None, None, None),
        P("elem", None, None),
        P("elem", None),
        P("elem", None),
        P("elem"),
        P("elem", None),
    )
    out_specs = (P(None, "dir", "elem"), P(None, "dir", "elem"))
    return jax.shard_map(
        functools.partial(on_device, n=mesh.shape["elem"]), mesh=mesh,
        in_specs=in_specs, out_specs=out_specs, check_vma=False)
```

```python
import functools

import jax
import jax.numpy as jnp
from jax import lax
from jax.experimental import pallas as pl
from jax.experimental.pallas import tpu as pltpu
from jax.sharding import PartitionSpec as P

MESH = pl.DeviceIdType.MESH
LANES = 128
PIECES = 2


def bit(value, place):
    return lax.rem(lax.div(value, 1 << place), 2)


def flip(value, mask):
    for place in range(mask.bit_length()):
        if mask >> place & 1:
            value = value + (1 << place) * (1 - 2 * bit(value, place))
    return value


def when(condition, body):
    if condition is True:
        body()
    elif condition is not False:
        pl.when(condition)(body)


def both(a, b):
    if a is False or b is False:
        return False
    if a is True:
        return b
    if b is True:
        return a
    return jnp.logical_and(a, b)


def march_kernel(n, hist_hbm, inc_hbm, z_hbm, zinv_hbm, basis_hbm, cols_hbm,
                 lags_hbm, counts_hbm,
                 dens_out, far_out,
                 ext, weights, basis, inc, slot_table, counts, dens0, part, far_in,
                 own_sem, table_sem, load_sem, ready, line_recv, hist_recv, hist_send,
                 dens_recv, far_recv, late_send):
    me = lax.axis_index("elem")
    _, rows, slots = slot_table.shape
    levels, dirs, width = hist_hbm.shape
    half = n // 2
    owned = far_out.shape[2]
    z, y = lax.div(me, 2), lax.rem(me, 2)
    partner = me + 1 - 2 * y
    barrier = pltpu.get_barrier_semaphore()
    tuned = half == 4
    top = half - 1
    crosses = both(tuned, both(z == half - 1, y == 1))
    crossed = both(tuned, both(z == 0, y == 0))
    opposite = flip(z, top) * 2 + 1 - y

    def line(k):
        return flip(z, k) * 2 + y

    def later(k):
        return bit(z, k.bit_length() - 1) == 0

    def signal(semaphore, target):
        pl.semaphore_signal(semaphore, inc=1, device_id={"elem": target}, device_id_type=MESH)

    earlier = y
    when(y == 0, lambda: signal(barrier, partner))
    for k in range(1, half):
        when(later(k), lambda: signal(barrier, line(k)))
        earlier = earlier + jnp.where(later(k), 0, 1)
    if tuned:
        when(crossed, lambda: signal(barrier, opposite))
        earlier = earlier + jnp.where(crosses, 1, 0)
    per = levels * rows
    own = [
        pltpu.make_async_copy(
            hist_hbm.at[:, :, pl.ds(row * LANES, LANES)],
            ext.at[pl.ds(me * per + row * levels, levels)], own_sem)
        for row in range(rows)]
    for copy in own:
        copy.start()
    when(me > 0, lambda: pl.semaphore_wait(barrier, earlier))
    for k in range(half - 1, 0, -1):
        when(jnp.logical_not(later(k)), lambda: signal(ready.at[k], line(k)))
    when(y == 1, lambda: signal(ready.at[0], partner))

    def block_copy(start, size, target, recv_sem):
        place = pl.ds(start, size)
        return pltpu.make_async_remote_copy(
            src_ref=ext.at[place], dst_ref=ext.at[place], send_sem=hist_send, recv_sem=recv_sem,
            device_id={"elem": target}, device_id_type=MESH)

    size = per // PIECES
    starts = [piece * size for piece in range(PIECES)]

    def along(k):
        for piece, start in enumerate(starts):
            block_copy(me * per + start, size, line(k), line_recv.at[k - 1, piece]).start()

    def along_in(k, relay=False):
        for piece, start in enumerate(starts):
            at = line(k) * per + start
            block_copy(at, size, partner, line_recv.at[k - 1, piece]).wait_recv()
            if relay:
                block_copy(at, size, partner, hist_recv).start()

    to_partner = block_copy(me * per, per, partner, hist_recv)
    cross = block_copy(me * per, per, opposite, hist_recv)

    def rest(blocks):
        return block_copy(0, blocks * per, partner, hist_recv)

    deep = z_hbm.shape[1]
    tables = [
        pltpu.make_async_copy(cols_hbm, slot_table.at[0], table_sem.at[0]),
        pltpu.make_async_copy(lags_hbm, slot_table.at[1], table_sem.at[0]),
        pltpu.make_async_copy(counts_hbm, counts, table_sem.at[1]),
    ]
    loads = [
        pltpu.make_async_copy(z_hbm, weights.at[:, pl.ds(0, deep)], load_sem.at[0]),
        pltpu.make_async_copy(zinv_hbm, weights.at[:, pl.ds(deep, LANES)], load_sem.at[0]),
        pltpu.make_async_copy(basis_hbm, basis, load_sem.at[1]),
        pltpu.make_async_copy(inc_hbm, inc, load_sem.at[2]),
    ]
    pltpu.make_async_copy(ext.at[pl.ds(0, per)], ext.at[pl.ds(0, per)], own_sem).wait()
    when(y == 1, lambda: to_partner.start())
    for k in range(1, half):
        when(jnp.logical_not(later(k)), lambda: along(k))
    when(crosses, lambda: cross.start())
    for load in tables + loads:
        load.start()

    middle = lax.rem(bit(z, 0) + bit(z, 1), 2) == 1
    if tuned:
        outer = jnp.logical_not(middle)
        order = [(0, True), (1, True), (3, middle), (2, True), (3, outer)]
    else:
        order = [(k, True) for k in range(half)]
    for k, chosen in order:
        def answer():
            pl.semaphore_wait(ready.at[k], 1)
            to_partner.start() if k == 0 else along(k)
        when(both(chosen, y == 0 if k == 0 else later(k)), answer)

    ext[n * per] = jnp.zeros((dirs, LANES), ext.dtype)
    dens0[n * rows] = jnp.zeros((dirs, LANES), dens0.dtype)
    passes = {k: True for k in range(1, half)}
    if tuned:
        passes[top] = jnp.logical_not(both(z == 0, y == 1))
        first = z == 0
        order = [(1, True), (3, jnp.logical_not(first)), (2, True), (3, first)]
    else:
        order = [(k, True) for k in range(1, half)]
    for k, chosen in order:
        def pass_on():
            along_in(k, relay=True)
        when(both(chosen, passes[k]), pass_on)
    pltpu.make_async_copy(slot_table, slot_table, table_sem.at[0]).wait()
    tables[2].wait()
    place0, place1, from_dens = [], [], []
    for row in range(rows):
        live = counts[row]
        for slot in range(slots):
            column, lag = slot_table[0, row, slot], slot_table[1, row, slot]
            lag = jnp.where(slot < live, lag, 0)
            newest = column * levels + lag - 1
            place0.append(jnp.where(lag > 0, newest, n * per))
            place1.append(jnp.where(lag > 1, newest - 1, n * per))
            from_dens.append(jnp.where(lag == 1, column, n * rows))

    if tuned:
        when(jnp.logical_not(passes[top]), lambda: along_in(top))
    rest(half).wait_recv()
    pltpu.make_async_copy(weights, weights, load_sem.at[0]).wait()
    for load in loads[2:]:
        load.wait()

    sums = []
    for row in range(rows):
        picked = []
        for at in range(row * slots, (row + 1) * slots):
            picked.append(jnp.concatenate([ext[place0[at]], ext[place1[at]]], axis=0))
        sums.append(jnp.dot(jnp.concatenate(picked, axis=1), weights[row, 0:deep],
                            preferred_element_type=jnp.float32))

    def density_of(step, row, history_sum):
        own_field = inc[step, :, row * LANES:(row + 1) * LANES].astype(jnp.float32)
        source = (own_field - history_sum).astype(jnp.bfloat16)
        return jnp.dot(source, weights[row, deep:], preferred_element_type=jnp.float32).astype(jnp.bfloat16)

    for row in range(rows):
        density = density_of(0, row, sums[row][0:dirs])
        dens0[me * rows + row] = density
        dens_out[0, :, row * LANES:(row + 1) * LANES] = density

    def send_density(mask):
        place = pl.ds(me * rows, rows)
        return pltpu.make_async_remote_copy(
            src_ref=dens0.at[place], dst_ref=dens0.at[place], send_sem=late_send, recv_sem=dens_recv,
            device_id={"elem": flip(me, mask)}, device_id_type=MESH)

    masks = list(range(n - 1, 0, -1))
    for mask in masks:
        send_density(mask).start()

    def send_far(step):
        for target in range(n):
            def send():
                pltpu.make_async_remote_copy(
                    src_ref=part.at[step, target * owned // LANES], dst_ref=far_in.at[step * n + me],
                    send_sem=late_send, recv_sem=far_recv,
                    device_id={"elem": target}, device_id_type=MESH).start()
            when(me != target, send)

    def arrived(buffer, count, semaphore):
        place = buffer.at[pl.ds(0, count)]
        pltpu.make_async_copy(place, place, semaphore).wait()

    def far_parts(step, density):
        value = jnp.dot(density, basis[...], preferred_element_type=jnp.float32)
        for tile in range(part.shape[1]):
            part[step, tile] = value[:, tile * LANES:(tile + 1) * LANES]

    far_parts(0, dens_out[0])
    send_far(0)
    arrived(dens0, (n - 1) * rows, dens_recv)
    for row in range(rows):
        picked = [dens0[from_dens[at]] for at in range(row * slots, (row + 1) * slots)]
        total = sums[row][dirs:2 * dirs] + jnp.dot(
            jnp.concatenate(picked, axis=1), weights[row, 0:deep], preferred_element_type=jnp.float32)
        dens_out[1, :, row * LANES:(row + 1) * LANES] = density_of(1, row, total)
    far_parts(1, dens_out[1])
    send_far(1)

    if tuned:
        fewer = jnp.logical_not(passes[top])
        when(crosses, lambda: rest(n).wait_send())
        when(fewer, lambda: rest(n - 2).wait_send())
        when(jnp.logical_not(jnp.logical_or(crosses, fewer)), lambda: rest(n - 1).wait_send())
    else:
        rest(n - 1).wait_send()

    shift = lax.rem(me * owned, LANES)
    steps = part.shape[0]
    arrived(far_in, steps * (n - 1), far_recv)
    for step in range(steps):
        far_in[step * n + me] = part[step, me * owned // LANES]
        total = far_in[step * n]
        for source in range(1, n):
            total = total + far_in[step * n + source]
        total = pltpu.roll(total, lax.rem(LANES - shift, LANES), 1)
        far_out[step] = total[:, 0:owned]
    arrived(ext, (n - 1) * (rows + 2 * steps), late_send)


def on_device(history, incident, ztiles, zinv, columns, lags, counts, basis, *, n):
    steps, dirs, width = incident.shape
    levels = history.shape[0]
    rows, slots, tile, _ = ztiles.shape
    coeffs = basis.shape[1]
    flat = ztiles.reshape(rows, slots * tile, tile)
    hbm = pl.BlockSpec(memory_space=pltpu.HBM)
    vmem = pl.BlockSpec(memory_space=pltpu.VMEM)
    bf16, f32 = jnp.bfloat16, jnp.float32
    dma = pltpu.SemaphoreType.DMA
    tiles = coeffs // LANES
    half = n // 2
    return pl.pallas_call(
        functools.partial(march_kernel, n),
        out_shape=(pltpu.VMEM((steps, dirs, width), bf16),
                   pltpu.VMEM((steps, dirs, coeffs // n), f32)),
        in_specs=[hbm] * 8,
        out_specs=(vmem, vmem),
        scratch_shapes=[
            pltpu.VMEM((n * levels * rows + 1, dirs, LANES), bf16),
            pltpu.VMEM((rows, (slots + 1) * tile, tile), bf16),
            pltpu.VMEM(basis.shape, bf16),
            pltpu.VMEM(incident.shape, bf16),
            pltpu.SMEM((2,) + columns.shape, jnp.int32),
            pltpu.SMEM(counts.shape, jnp.int32),
            pltpu.VMEM((n * rows + 1, dirs, LANES), bf16),
            pltpu.VMEM((steps, tiles, dirs, LANES), f32),
            pltpu.VMEM((steps * n, dirs, LANES), f32),
            dma, dma((2,)), dma((3,)),
            pltpu.SemaphoreType.REGULAR((half,)), dma((half - 1, PIECES)),
            dma, dma, dma, dma, dma,
        ],
        compiler_params=pltpu.CompilerParams(
            collective_id=0, has_side_effects=True, vmem_limit_bytes=32 * 1024 * 1024),
    )(*(pltpu.with_memory_space_constraint(x, pltpu.HBM)
        for x in (history, incident, flat, zinv, basis, columns, lags, counts)))


def solution(mesh):
    in_specs = (
        P(None, "dir", "elem"),
        P(None, "dir", "elem"),
        P("elem", None, None, None),
        P("elem", None, None),
        P("elem", None),
        P("elem", None),
        P("elem"),
        P("elem", None),
    )
    out_specs = (P(None, "dir", "elem"), P(None, "dir", "elem"))
    return jax.shard_map(
        functools.partial(on_device, n=mesh.shape["elem"]), mesh=mesh,
        in_specs=in_specs, out_specs=out_specs, check_vma=False)
```

```python
import functools

import jax
import jax.numpy as jnp
from jax import lax
from jax.experimental import pallas as pl
from jax.experimental.pallas import tpu as pltpu
from jax.sharding import PartitionSpec as P

MESH = pl.DeviceIdType.MESH
LANES = 128
PIECES = 2


def bit(value, place):
    return lax.rem(lax.div(value, 1 << place), 2)


def flip(value, mask):
    for place in range(mask.bit_length()):
        if mask >> place & 1:
            value = value + (1 << place) * (1 - 2 * bit(value, place))
    return value


def when(condition, body):
    if condition is True:
        body()
    elif condition is not False:
        pl.when(condition)(body)


def both(a, b):
    if a is False or b is False:
        return False
    if a is True:
        return b
    if b is True:
        return a
    return jnp.logical_and(a, b)


def march_kernel(n, hist_hbm, inc_hbm, z_hbm, zinv_hbm, basis_hbm, cols_hbm,
                 lags_hbm, counts_hbm,
                 dens_out, far_out,
                 ext, weights, basis, inc, slot_table, counts, dens0, part, far_in,
                 own_sem, table_sem, load_sem, ready, line_recv, hist_recv, hist_send,
                 dens_recv, far_recv, late_send):
    me = lax.axis_index("elem")
    _, rows, slots = slot_table.shape
    levels, dirs, width = hist_hbm.shape
    half = n // 2
    owned = far_out.shape[2]
    z, y = lax.div(me, 2), lax.rem(me, 2)
    partner = me + 1 - 2 * y
    barrier = pltpu.get_barrier_semaphore()
    tuned = half == 4
    top = half - 1
    crosses = both(tuned, both(z == half - 1, y == 1))
    crossed = both(tuned, both(z == 0, y == 0))
    opposite = flip(z, top) * 2 + 1 - y

    def line(k):
        return flip(z, k) * 2 + y

    def later(k):
        return bit(z, k.bit_length() - 1) == 0

    def signal(semaphore, target):
        pl.semaphore_signal(semaphore, inc=1, device_id={"elem": target}, device_id_type=MESH)

    earlier = y
    when(y == 0, lambda: signal(barrier, partner))
    for k in range(1, half):
        when(later(k), lambda: signal(barrier, line(k)))
        earlier = earlier + jnp.where(later(k), 0, 1)
    if tuned:
        when(crossed, lambda: signal(barrier, opposite))
        earlier = earlier + jnp.where(crosses, 1, 0)
    per = levels * rows
    own = [
        pltpu.make_async_copy(
            hist_hbm.at[:, :, pl.ds(row * LANES, LANES)],
            ext.at[pl.ds(me * per + row * levels, levels)], own_sem)
        for row in range(rows)]
    for copy in own:
        copy.start()
    when(me > 0, lambda: pl.semaphore_wait(barrier, earlier))
    for k in range(half - 1, 0, -1):
        when(jnp.logical_not(later(k)), lambda: signal(ready.at[k], line(k)))
    when(y == 1, lambda: signal(ready.at[0], partner))

    def block_copy(start, size, target, recv_sem):
        place = pl.ds(start, size)
        return pltpu.make_async_remote_copy(
            src_ref=ext.at[place], dst_ref=ext.at[place], send_sem=hist_send, recv_sem=recv_sem,
            device_id={"elem": target}, device_id_type=MESH)

    size = per // PIECES
    starts = [piece * size for piece in range(PIECES)]

    def along(k):
        for piece, start in enumerate(starts):
            block_copy(me * per + start, size, line(k), line_recv.at[k - 1, piece]).start()

    def along_in(k, relay=False):
        for piece, start in enumerate(starts):
            at = line(k) * per + start
            block_copy(at, size, partner, line_recv.at[k - 1, piece]).wait_recv()
            if relay:
                block_copy(at, size, partner, hist_recv).start()

    to_partner = block_copy(me * per, per, partner, hist_recv)
    cross = block_copy(me * per, per, opposite, hist_recv)

    def rest(blocks):
        return block_copy(0, blocks * per, partner, hist_recv)

    deep = z_hbm.shape[1]
    tables = [
        pltpu.make_async_copy(cols_hbm, slot_table.at[0], table_sem.at[0]),
        pltpu.make_async_copy(lags_hbm, slot_table.at[1], table_sem.at[0]),
        pltpu.make_async_copy(counts_hbm, counts, table_sem.at[1]),
    ]
    loads = [
        pltpu.make_async_copy(z_hbm, weights.at[:, pl.ds(0, deep)], load_sem.at[0]),
        pltpu.make_async_copy(zinv_hbm, weights.at[:, pl.ds(deep, LANES)], load_sem.at[0]),
        pltpu.make_async_copy(basis_hbm, basis, load_sem.at[1]),
        pltpu.make_async_copy(inc_hbm, inc, load_sem.at[2]),
    ]
    pltpu.make_async_copy(ext.at[pl.ds(0, per)], ext.at[pl.ds(0, per)], own_sem).wait()
    when(y == 1, lambda: to_partner.start())
    for k in range(1, half):
        when(jnp.logical_not(later(k)), lambda: along(k))
    when(crosses, lambda: cross.start())
    for load in tables + loads:
        load.start()

    middle = lax.rem(bit(z, 0) + bit(z, 1), 2) == 1
    if tuned:
        outer = jnp.logical_not(middle)
        order = [(0, True), (1, True), (3, middle), (2, True), (3, outer)]
    else:
        order = [(k, True) for k in range(half)]
    for k, chosen in order:
        def answer():
            pl.semaphore_wait(ready.at[k], 1)
            to_partner.start() if k == 0 else along(k)
        when(both(chosen, y == 0 if k == 0 else later(k)), answer)

    ext[n * per] = jnp.zeros((dirs, LANES), ext.dtype)
    dens0[n * rows] = jnp.zeros((dirs, LANES), dens0.dtype)
    passes = {k: True for k in range(1, half)}
    if tuned:
        passes[top] = jnp.logical_not(both(z == 0, y == 1))
        first = z == 0
        order = [(1, True), (3, jnp.logical_not(first)), (2, True), (3, first)]
    else:
        order = [(k, True) for k in range(1, half)]
    for k, chosen in order:
        def pass_on():
            along_in(k, relay=True)
        when(both(chosen, passes[k]), pass_on)
    pltpu.make_async_copy(slot_table, slot_table, table_sem.at[0]).wait()
    tables[2].wait()
    place0, place1, from_dens = [], [], []
    for row in range(rows):
        live = counts[row]
        for slot in range(slots):
            column, lag = slot_table[0, row, slot], slot_table[1, row, slot]
            lag = jnp.where(slot < live, lag, 0)
            newest = column * levels + lag - 1
            place0.append(jnp.where(lag > 0, newest, n * per))
            place1.append(jnp.where(lag > 1, newest - 1, n * per))
            from_dens.append(jnp.where(lag == 1, column, n * rows))

    if tuned:
        when(jnp.logical_not(passes[top]), lambda: along_in(top))
    rest(half).wait_recv()
    pltpu.make_async_copy(weights, weights, load_sem.at[0]).wait()
    for load in loads[2:]:
        load.wait()

    sums = []
    for row in range(rows):
        picked = []
        for at in range(row * slots, (row + 1) * slots):
            picked.append(jnp.concatenate([ext[place0[at]], ext[place1[at]]], axis=0))
        sums.append(jnp.dot(jnp.concatenate(picked, axis=1), weights[row, 0:deep],
                            preferred_element_type=jnp.float32))

    def density_of(step, row, history_sum):
        own_field = inc[step, :, row * LANES:(row + 1) * LANES].astype(jnp.float32)
        source = (own_field - history_sum).astype(jnp.bfloat16)
        return jnp.dot(source, weights[row, deep:], preferred_element_type=jnp.float32).astype(jnp.bfloat16)

    for row in range(rows):
        density = density_of(0, row, sums[row][0:dirs])
        dens0[me * rows + row] = density
        dens_out[0, :, row * LANES:(row + 1) * LANES] = density

    def send_density(mask):
        place = pl.ds(me * rows, rows)
        return pltpu.make_async_remote_copy(
            src_ref=dens0.at[place], dst_ref=dens0.at[place], send_sem=late_send, recv_sem=dens_recv,
            device_id={"elem": flip(me, mask)}, device_id_type=MESH)

    masks = list(range(n - 1, 0, -1))
    for mask in masks:
        send_density(mask).start()

    def send_far(step):
        for target in range(n):
            def send():
                pltpu.make_async_remote_copy(
                    src_ref=part.at[step, target * owned // LANES], dst_ref=far_in.at[step * n + me],
                    send_sem=late_send, recv_sem=far_recv,
                    device_id={"elem": target}, device_id_type=MESH).start()
            when(me != target, send)

    def arrived(buffer, count, semaphore):
        place = buffer.at[pl.ds(0, count)]
        pltpu.make_async_copy(place, place, semaphore).wait()

    def far_parts(step, density):
        value = jnp.dot(density, basis[...], preferred_element_type=jnp.float32)
        for tile in range(part.shape[1]):
            part[step, tile] = value[:, tile * LANES:(tile + 1) * LANES]

    far_parts(0, dens_out[0])
    send_far(0)
    arrived(dens0, (n - 1) * rows, dens_recv)
    for row in range(rows):
        picked = [dens0[from_dens[at]] for at in range(row * slots, (row + 1) * slots)]
        total = sums[row][dirs:2 * dirs] + jnp.dot(
            jnp.concatenate(picked, axis=1), weights[row, 0:deep], preferred_element_type=jnp.float32)
        dens_out[1, :, row * LANES:(row + 1) * LANES] = density_of(1, row, total)
    far_parts(1, dens_out[1])
    send_far(1)

    if tuned:
        fewer = jnp.logical_not(passes[top])
        when(crosses, lambda: rest(n).wait_send())
        when(fewer, lambda: rest(n - 2).wait_send())
        when(jnp.logical_not(jnp.logical_or(crosses, fewer)), lambda: rest(n - 1).wait_send())
    else:
        rest(n - 1).wait_send()

    shift = lax.rem(me * owned, LANES)
    steps = part.shape[0]
    arrived(far_in, steps * (n - 1), far_recv)
    for step in range(steps):
        far_in[step * n + me] = part[step, me * owned // LANES]
        total = far_in[step * n]
        for source in range(1, n):
            total = total + far_in[step * n + source]
        total = pltpu.roll(total, lax.rem(LANES - shift, LANES), 1)
        far_out[step] = total[:, 0:owned]
    arrived(ext, (n - 1) * (rows + 2 * steps), late_send)


def store_kernel(dens, far, dens_out, far_out):
    dens_out[...] = dens[...]
    far_out[...] = far[...]


def on_device(history, incident, ztiles, zinv, columns, lags, counts, basis, *, n):
    steps, dirs, width = incident.shape
    levels = history.shape[0]
    rows, slots, tile, _ = ztiles.shape
    coeffs = basis.shape[1]
    flat = ztiles.reshape(rows, slots * tile, tile)
    hbm = pl.BlockSpec(memory_space=pltpu.HBM)
    vmem = pl.BlockSpec(memory_space=pltpu.VMEM)
    bf16, f32 = jnp.bfloat16, jnp.float32
    dma = pltpu.SemaphoreType.DMA
    tiles = coeffs // LANES
    half = n // 2
    results = pl.pallas_call(
        functools.partial(march_kernel, n),
        out_shape=(pltpu.VMEM((steps, dirs, width), bf16),
                   pltpu.VMEM((steps, dirs, coeffs // n), f32)),
        in_specs=[hbm] * 8,
        out_specs=(vmem, vmem),
        scratch_shapes=[
            pltpu.VMEM((n * levels * rows + 1, dirs, LANES), bf16),
            pltpu.VMEM((rows, (slots + 1) * tile, tile), bf16),
            pltpu.VMEM(basis.shape, bf16),
            pltpu.VMEM(incident.shape, bf16),
            pltpu.SMEM((2,) + columns.shape, jnp.int32),
            pltpu.SMEM(counts.shape, jnp.int32),
            pltpu.VMEM((n * rows + 1, dirs, LANES), bf16),
            pltpu.VMEM((steps, tiles, dirs, LANES), f32),
            pltpu.VMEM((steps * n, dirs, LANES), f32),
            dma, dma((2,)), dma((3,)),
            pltpu.SemaphoreType.REGULAR((half,)), dma((half - 1, PIECES)),
            dma, dma, dma, dma, dma,
        ],
        compiler_params=pltpu.CompilerParams(
            collective_id=0, has_side_effects=True, vmem_limit_bytes=32 * 1024 * 1024),
    )(*(pltpu.with_memory_space_constraint(x, pltpu.HBM)
        for x in (history, incident, flat, zinv, basis, columns, lags, counts)))
    return pl.pallas_call(
        store_kernel,
        out_shape=tuple(jax.ShapeDtypeStruct(x.shape, x.dtype) for x in results),
        in_specs=[vmem, vmem],
        out_specs=(vmem, vmem),
    )(*(pltpu.with_memory_space_constraint(x, pltpu.VMEM) for x in results))


def solution(mesh):
    in_specs = (
        P(None, "dir", "elem"),
        P(None, "dir", "elem"),
        P("elem", None, None, None),
        P("elem", None, None),
        P("elem", None),
        P("elem", None),
        P("elem"),
        P("elem", None),
    )
    out_specs = (P(None, "dir", "elem"), P(None, "dir", "elem"))
    return jax.shard_map(
        functools.partial(on_device, n=mesh.shape["elem"]), mesh=mesh,
        in_specs=in_specs, out_specs=out_specs, check_vma=False)
```

```python
import functools

import jax
import jax.numpy as jnp
from jax import lax
from jax.experimental import pallas as pl
from jax.experimental.pallas import tpu as pltpu
from jax.sharding import PartitionSpec as P

MESH = pl.DeviceIdType.MESH
LANES = 128


def bit(value, place):
    return lax.rem(lax.div(value, 1 << place), 2)


def flip(value, mask):
    for place in range(mask.bit_length()):
        if mask >> place & 1:
            value = value + (1 << place) * (1 - 2 * bit(value, place))
    return value


def when(condition, body):
    if condition is True:
        body()
    elif condition is not False:
        pl.when(condition)(body)


def both(a, b):
    if a is False or b is False:
        return False
    if a is True:
        return b
    if b is True:
        return a
    return jnp.logical_and(a, b)


def march_kernel(n, hist_hbm, inc_hbm, z_hbm, zinv_hbm, basis_hbm, cols_hbm,
                 lags_hbm, counts_hbm,
                 dens_out, far_out,
                 ext, weights, basis, inc, slot_table, counts, dens0, part, far_in,
                 own_sem, table_sem, load_sem, ready, line_recv, hist_recv, hist_send,
                 dens_recv, far_recv, late_send):
    me = lax.axis_index("elem")
    _, rows, slots = slot_table.shape
    levels, dirs, width = hist_hbm.shape
    half = n // 2
    owned = far_out.shape[2]
    z, y = lax.div(me, 2), lax.rem(me, 2)
    partner = me + 1 - 2 * y
    barrier = pltpu.get_barrier_semaphore()
    tuned = half == 4
    top = half - 1
    crosses = both(tuned, both(z == half - 1, y == 1))
    crossed = both(tuned, both(z == 0, y == 0))
    opposite = flip(z, top) * 2 + 1 - y

    def line(k):
        return flip(z, k) * 2 + y

    def later(k):
        return bit(z, k.bit_length() - 1) == 0

    def signal(semaphore, target):
        pl.semaphore_signal(semaphore, inc=1, device_id={"elem": target}, device_id_type=MESH)

    earlier = y
    when(y == 0, lambda: signal(barrier, partner))
    for k in range(1, half):
        when(later(k), lambda: signal(barrier, line(k)))
        earlier = earlier + jnp.where(later(k), 0, 1)
    if tuned:
        when(crossed, lambda: signal(barrier, opposite))
        earlier = earlier + jnp.where(crosses, 1, 0)
    per = levels * rows
    own = [
        pltpu.make_async_copy(
            hist_hbm.at[:, :, pl.ds(row * LANES, LANES)],
            ext.at[pl.ds(me * per + row * levels, levels)], own_sem)
        for row in range(rows)]
    for copy in own:
        copy.start()
    when(me > 0, lambda: pl.semaphore_wait(barrier, earlier))
    for k in range(half - 1, 0, -1):
        when(jnp.logical_not(later(k)), lambda: signal(ready.at[k], line(k)))
    when(y == 1, lambda: signal(ready.at[0], partner))

    def block_copy(start, size, target, recv_sem):
        place = pl.ds(start, size)
        return pltpu.make_async_remote_copy(
            src_ref=ext.at[place], dst_ref=ext.at[place], send_sem=hist_send, recv_sem=recv_sem,
            device_id={"elem": target}, device_id_type=MESH)

    size = levels
    starts = [row * levels for row in range(rows)]

    def along(k, piece_list=range(rows)):
        for piece in piece_list:
            block_copy(me * per + starts[piece], size, line(k), line_recv.at[k - 1, piece]).start()

    def along_in(k, relay=False):
        for piece, start in enumerate(starts):
            at = line(k) * per + start
            block_copy(at, size, partner, line_recv.at[k - 1, piece]).wait_recv()
            if relay:
                block_copy(at, size, partner, hist_recv).start()

    to_partner = block_copy(me * per, per, partner, hist_recv)
    cross = block_copy(me * per, per, opposite, hist_recv)

    def rest(blocks):
        return block_copy(0, blocks * per, partner, hist_recv)

    deep = z_hbm.shape[1]
    tables = [
        pltpu.make_async_copy(cols_hbm, slot_table.at[0], table_sem.at[0]),
        pltpu.make_async_copy(lags_hbm, slot_table.at[1], table_sem.at[0]),
        pltpu.make_async_copy(counts_hbm, counts, table_sem.at[1]),
    ]
    loads = [
        pltpu.make_async_copy(z_hbm, weights.at[:, pl.ds(0, deep)], load_sem.at[0]),
        pltpu.make_async_copy(zinv_hbm, weights.at[:, pl.ds(deep, LANES)], load_sem.at[0]),
        pltpu.make_async_copy(basis_hbm, basis, load_sem.at[1]),
        pltpu.make_async_copy(inc_hbm, inc, load_sem.at[2]),
    ]
    pltpu.make_async_copy(ext.at[pl.ds(0, per)], ext.at[pl.ds(0, per)], own_sem).wait()
    when(y == 1, lambda: to_partner.start())
    for k in range(1, half):
        when(jnp.logical_not(later(k)), lambda: along(k))
    when(crosses, lambda: cross.start())
    for load in tables + loads:
        load.start()

    middle = lax.rem(bit(z, 0) + bit(z, 1), 2) == 1
    if tuned:
        outer = jnp.logical_not(middle)
        order = [(0, True), (1, True), (3, middle), (2, True), (3, outer)]
    else:
        order = [(k, True) for k in range(half)]
    for k, chosen in order:
        def answer():
            pl.semaphore_wait(ready.at[k], 1)
            to_partner.start() if k == 0 else along(k)
        when(both(chosen, y == 0 if k == 0 else later(k)), answer)

    ext[n * per] = jnp.zeros((dirs, LANES), ext.dtype)
    dens0[n * rows] = jnp.zeros((dirs, LANES), dens0.dtype)
    passes = {k: True for k in range(1, half)}
    if tuned:
        passes[top] = jnp.logical_not(both(z == 0, y == 1))
        first = z == 0
        order = [(1, True), (3, jnp.logical_not(first)), (2, True), (3, first)]
    else:
        order = [(k, True) for k in range(1, half)]
    for k, chosen in order:
        def pass_on():
            along_in(k, relay=True)
        when(both(chosen, passes[k]), pass_on)
    pltpu.make_async_copy(slot_table, slot_table, table_sem.at[0]).wait()
    tables[2].wait()
    place0, place1, from_dens = [], [], []
    for row in range(rows):
        live = counts[row]
        for slot in range(slots):
            column, lag = slot_table[0, row, slot], slot_table[1, row, slot]
            lag = jnp.where(slot < live, lag, 0)
            newest = column * levels + lag - 1
            place0.append(jnp.where(lag > 0, newest, n * per))
            place1.append(jnp.where(lag > 1, newest - 1, n * per))
            from_dens.append(jnp.where(lag == 1, column, n * rows))

    if tuned:
        when(jnp.logical_not(passes[top]), lambda: along_in(top))
    rest(half).wait_recv()
    pltpu.make_async_copy(weights, weights, load_sem.at[0]).wait()
    for load in loads[2:]:
        load.wait()

    sums = []
    for row in range(rows):
        picked = []
        for at in range(row * slots, (row + 1) * slots):
            picked.append(jnp.concatenate([ext[place0[at]], ext[place1[at]]], axis=0))
        sums.append(jnp.dot(jnp.concatenate(picked, axis=1), weights[row, 0:deep],
                            preferred_element_type=jnp.float32))

    def density_of(step, row, history_sum):
        own_field = inc[step, :, row * LANES:(row + 1) * LANES].astype(jnp.float32)
        source = (own_field - history_sum).astype(jnp.bfloat16)
        return jnp.dot(source, weights[row, deep:], preferred_element_type=jnp.float32).astype(jnp.bfloat16)

    for row in range(rows):
        density = density_of(0, row, sums[row][0:dirs])
        dens0[me * rows + row] = density
        dens_out[0, :, row * LANES:(row + 1) * LANES] = density

    def send_density(mask):
        place = pl.ds(me * rows, rows)
        return pltpu.make_async_remote_copy(
            src_ref=dens0.at[place], dst_ref=dens0.at[place], send_sem=late_send, recv_sem=dens_recv,
            device_id={"elem": flip(me, mask)}, device_id_type=MESH)

    masks = list(range(n - 1, 0, -1))
    for mask in masks:
        send_density(mask).start()

    def send_far(step):
        for target in range(n):
            def send():
                pltpu.make_async_remote_copy(
                    src_ref=part.at[step, target * owned // LANES], dst_ref=far_in.at[step * n + me],
                    send_sem=late_send, recv_sem=far_recv,
                    device_id={"elem": target}, device_id_type=MESH).start()
            when(me != target, send)

    def arrived(buffer, count, semaphore):
        place = buffer.at[pl.ds(0, count)]
        pltpu.make_async_copy(place, place, semaphore).wait()

    def far_parts(step, density):
        value = jnp.dot(density, basis[...], preferred_element_type=jnp.float32)
        for tile in range(part.shape[1]):
            part[step, tile] = value[:, tile * LANES:(tile + 1) * LANES]

    far_parts(0, dens_out[0])
    send_far(0)
    arrived(dens0, (n - 1) * rows, dens_recv)
    for row in range(rows):
        picked = [dens0[from_dens[at]] for at in range(row * slots, (row + 1) * slots)]
        total = sums[row][dirs:2 * dirs] + jnp.dot(
            jnp.concatenate(picked, axis=1), weights[row, 0:deep], preferred_element_type=jnp.float32)
        dens_out[1, :, row * LANES:(row + 1) * LANES] = density_of(1, row, total)
    far_parts(1, dens_out[1])
    send_far(1)

    if tuned:
        fewer = jnp.logical_not(passes[top])
        when(crosses, lambda: rest(n).wait_send())
        when(fewer, lambda: rest(n - 2).wait_send())
        when(jnp.logical_not(jnp.logical_or(crosses, fewer)), lambda: rest(n - 1).wait_send())
    else:
        rest(n - 1).wait_send()

    shift = lax.rem(me * owned, LANES)
    steps = part.shape[0]
    arrived(far_in, steps * (n - 1), far_recv)
    for step in range(steps):
        far_in[step * n + me] = part[step, me * owned // LANES]
        total = far_in[step * n]
        for source in range(1, n):
            total = total + far_in[step * n + source]
        total = pltpu.roll(total, lax.rem(LANES - shift, LANES), 1)
        far_out[step] = total[:, 0:owned]
    arrived(ext, (n - 1) * (rows + 2 * steps), late_send)


def store_kernel(dens, far, dens_out, far_out):
    dens_out[...] = dens[...]
    far_out[...] = far[...]


def on_device(history, incident, ztiles, zinv, columns, lags, counts, basis, *, n):
    steps, dirs, width = incident.shape
    levels = history.shape[0]
    rows, slots, tile, _ = ztiles.shape
    coeffs = basis.shape[1]
    flat = ztiles.reshape(rows, slots * tile, tile)
    hbm = pl.BlockSpec(memory_space=pltpu.HBM)
    vmem = pl.BlockSpec(memory_space=pltpu.VMEM)
    bf16, f32 = jnp.bfloat16, jnp.float32
    dma = pltpu.SemaphoreType.DMA
    tiles = coeffs // LANES
    half = n // 2
    results = pl.pallas_call(
        functools.partial(march_kernel, n),
        out_shape=(pltpu.VMEM((steps, dirs, width), bf16),
                   pltpu.VMEM((steps, dirs, coeffs // n), f32)),
        in_specs=[hbm] * 8,
        out_specs=(vmem, vmem),
        scratch_shapes=[
            pltpu.VMEM((n * levels * rows + 1, dirs, LANES), bf16),
            pltpu.VMEM((rows, (slots + 1) * tile, tile), bf16),
            pltpu.VMEM(basis.shape, bf16),
            pltpu.VMEM(incident.shape, bf16),
            pltpu.SMEM((2,) + columns.shape, jnp.int32),
            pltpu.SMEM(counts.shape, jnp.int32),
            pltpu.VMEM((n * rows + 1, dirs, LANES), bf16),
            pltpu.VMEM((steps, tiles, dirs, LANES), f32),
            pltpu.VMEM((steps * n, dirs, LANES), f32),
            dma, dma((2,)), dma((3,)),
            pltpu.SemaphoreType.REGULAR((half,)), dma((half - 1, rows)),
            dma, dma, dma, dma, dma,
        ],
        compiler_params=pltpu.CompilerParams(
            collective_id=0, has_side_effects=True, vmem_limit_bytes=32 * 1024 * 1024),
    )(*(pltpu.with_memory_space_constraint(x, pltpu.HBM)
        for x in (history, incident, flat, zinv, basis, columns, lags, counts)))
    return pl.pallas_call(
        store_kernel,
        out_shape=tuple(jax.ShapeDtypeStruct(x.shape, x.dtype) for x in results),
        in_specs=[vmem, vmem],
        out_specs=(vmem, vmem),
    )(*(pltpu.with_memory_space_constraint(x, pltpu.VMEM) for x in results))


def solution(mesh):
    in_specs = (
        P(None, "dir", "elem"),
        P(None, "dir", "elem"),
        P("elem", None, None, None),
        P("elem", None, None),
        P("elem", None),
        P("elem", None),
        P("elem"),
        P("elem", None),
    )
    out_specs = (P(None, "dir", "elem"), P(None, "dir", "elem"))
    return jax.shard_map(
        functools.partial(on_device, n=mesh.shape["elem"]), mesh=mesh,
        in_specs=in_specs, out_specs=out_specs, check_vma=False)
```
